128 devices in a mesh: orb: 128 (over z, x, y, core).
Axes of the slice: x: 4, y: 4, z: 4, core: 2. Of those that a mesh axis runs over, the one named last changes fastest.
Arguments:
- slabs: float32 [256, 384, 768], P('orb'), may hold values from -1.2 to 1.2
- amplitudes: float32 [1024, 384, 384], P('orb'), may hold values from -6 to 6
- intersections: float32 [1024, 3, 384, 384], P('orb'), may hold values from -0.3125 to 0.3125
- fock_coupling: float32 [1024, 3], P('orb'), may hold values from -0.9 to 0.9
- virt_energy: float32 [1024, 384], P('orb'), may hold values from 0.4 to 4
- occ_pair_energy: float32 [1024], P('orb'), may hold values from -2.4 to -0.4
- pair_orbs: int32 [1024, 2], P('orb'), may hold values from 0 to 255, as said below
- couplings: int32 [1024, 3], P('orb'), may hold values from 0 to 1023, as said below
Outputs:
- updated_amplitudes: float32 [1024, 384, 384], P('orb')
The draws below stay inside these ranges and needn't reach their ends.
Inputs may be any that keep to these rules, and one draw needn't show every extreme that they name: `pair_orbs`: row p holds orbitals (i, j), i != j. A device's block of 8 rows has i among that device's own 2 orbitals (rows of its block of slabs) and j among the orbitals of a device at most 2 away along the axis, counted without wrapping (the first and last devices are not neighbours here); every device's block names orbitals of some device 2 away and of some device next to it. `couplings`: entry (p, c) is a pair coupled to pair p. For c = 0 it is a pair in the block of the device before p's owner, and for c = 1 a pair in the block of the device after it. The axis closes: before the first device comes the last one, and after the last comes the first. Over one device's block of 8 rows, column 0 names exactly 4 distinct pairs, and so does column 1. For c = 2 it is another pair of p's own block.
All inputs are finite; a program needn't handle non-finite values.
Results may differ from the reference program's by a relative error of at most 0.0001.
Values sent between devices are 32-bit elements; how exact they have to be, the bound alone decides.
A program may use at most 192 MiB of HBM per device.

```python
import math
import jax
import jax.numpy as jnp
from jax import lax

NV = 384
NQ = 768
O_DEV = 2
P_DEV = 8
COUP = 3
REACH = 2
ITERS = 2
NOCC = 256
PAIRS = 1024


def draw_pair_orbs(key, part):
    device_count = PAIRS // P_DEV
    keys = jax.random.split(jax.random.fold_in(key, 101), 5)
    device = jnp.arange(device_count, dtype=jnp.int32)[:, None]
    slot = jnp.arange(P_DEV, dtype=jnp.int32)[None, :]
    fixed_offsets = jnp.array([-REACH, REACH, -1, 1], jnp.int32)
    shape = (device_count, P_DEV)
    magnitude = jax.random.randint(keys[0], shape, 1, REACH + 1)
    direction = 2 * jax.random.randint(keys[1], shape, 0, 2) - 1
    base = jnp.where(slot < 4, fixed_offsets[jnp.minimum(slot, 3)], magnitude * direction)
    scores = jax.random.randint(keys[2], shape, 0, 1 << 20) * P_DEV + slot
    order = jnp.argsort(scores, axis=1)
    offsets = jnp.take_along_axis(base, order, axis=1)
    target = device + offsets
    target = jnp.where((target < 0) | (target >= device_count), device - offsets, target)
    first = device * O_DEV + jax.random.randint(keys[3], shape, 0, O_DEV)
    second = target * O_DEV + jax.random.randint(keys[4], shape, 0, O_DEV)
    return jnp.stack([first, second], axis=-1).reshape(PAIRS, 2).astype(jnp.int32)


def draw_couplings(key, part):
    device_count = PAIRS // P_DEV
    half_count = P_DEV // 2
    keys = jax.random.split(jax.random.fold_in(key, 202), 3)
    device = jnp.arange(device_count, dtype=jnp.int32)[:, None, None]
    slot = jnp.arange(P_DEV, dtype=jnp.int32)[None, :, None]
    column = jnp.arange(COUP, dtype=jnp.int32)[None, None, :]
    side = jnp.where(column == 0, -1, jnp.where(column == 1, 1, 0))
    target = (device + side) % device_count
    subset_scores = jax.random.randint(keys[0], (device_count, COUP, P_DEV), 0, 1 << 20) * P_DEV + jnp.arange(P_DEV, dtype=jnp.int32)
    subset = jnp.argsort(subset_scores, axis=2).astype(jnp.int32)
    pick_scores = jax.random.randint(keys[1], (device_count, COUP, P_DEV), 0, 1 << 20) * P_DEV + jnp.arange(P_DEV, dtype=jnp.int32)
    pick_order = (jnp.argsort(pick_scores, axis=2) % half_count).astype(jnp.int32)
    chosen = jnp.take_along_axis(subset, pick_order, axis=2)
    chosen = jnp.transpose(chosen, (0, 2, 1))
    other = (slot + 1 + jax.random.randint(keys[2], (device_count, P_DEV, COUP), 0, P_DEV - 1)) % P_DEV
    within = jnp.where(side == 0, other, chosen)
    return (target * P_DEV + within).reshape(PAIRS, COUP).astype(jnp.int32)


def block_scale(stream_key, dims, shards, least, largest):
    gain = 1.0
    for dim, shards_of in shards:
        steps = jax.random.uniform(jax.random.fold_in(jax.random.fold_in(stream_key, 6), dim), (shards_of,), jnp.float32, least / len(shards), largest / len(shards))
        gain = gain * jnp.repeat(jnp.exp(steps), dims[dim] // shards_of).reshape((-1,) + (1,) * (len(dims) - 1 - dim))
    return gain


def centred(rng, shape, deviation, reach, cuts=(), held_as=jnp.bfloat16):
    values = deviation * jax.random.normal(rng, shape, jnp.float32)
    if cuts:
        values = values * block_scale(rng, shape, cuts, -0.22, 0.18)
    return jnp.clip(values, -reach, reach).astype(held_as)


def setup_inputs(seed: int = 0) -> dict:
    seeds = jax.random.split(jax.random.key(seed), 9)
    return {
        "slabs": centred(seeds[0], (NOCC, NV, NQ), 0.19, 1.2, ((0, 128),), jnp.float32),
        "amplitudes": centred(seeds[1], (PAIRS, NV, NV), 1.0, 6.0, ((0, 128),), jnp.float32),
        "intersections": centred(seeds[2], (PAIRS, COUP, NV, NV), NV ** -0.5, 0.3125, ((0, 128),), jnp.float32),
        "fock_coupling": jnp.clip(jax.random.uniform(seeds[3], (PAIRS, COUP), jnp.float32, -0.9, 0.9) * block_scale(seeds[3], (PAIRS, COUP), ((0, 128),), -0.4, 0.0), -0.9, 0.9),
        "virt_energy": jnp.clip(jnp.exp(math.log(4.0) - 2.3025851 * jax.random.uniform(seeds[4], (PAIRS, NV), jnp.float32) ** block_scale(seeds[4], (PAIRS, NV), ((0, 128),), -0.2, 0.2)), 0.4, 4.0),
        "occ_pair_energy": jnp.clip(-2.4 + 2 * jax.random.uniform(seeds[5], (PAIRS,), jnp.float32) ** block_scale(seeds[5], (PAIRS,), ((0, 128),), -0.2, 0.2), -2.4, -0.4),
        "pair_orbs": draw_pair_orbs(jax.random.fold_in(seeds[8], 71), 0),
        "couplings": draw_couplings(jax.random.fold_in(seeds[8], 71), 0),
    }


highest = lax.Precision.HIGHEST


def pair_integrals(slabs, pair_orbs):
    def one_pair(pair):
        left = slabs[pair[0]]
        right = slabs[pair[1]]
        return jnp.dot(left, right.T, precision=highest, preferred_element_type=jnp.float32)

    return lax.map(one_pair, pair_orbs)


def reference(slabs, amplitudes, intersections, fock_coupling, virt_energy, occ_pair_energy, pair_orbs, couplings):
    integrals = pair_integrals(slabs, pair_orbs)
    current = amplitudes
    for step in range(ITERS):
        def update(row):
            coupled_rows, gains, intersection, integral, virtual, occupied, own = row
            coupled = jnp.zeros((NV, NV), jnp.float32)
            for column in range(COUP):
                picked = current[coupled_rows[column]]
                half = jnp.dot(intersection[column], picked, precision=highest, preferred_element_type=jnp.float32)
                coupled = coupled + gains[column] * jnp.dot(half, intersection[column].T, precision=highest, preferred_element_type=jnp.float32)
            denominator = virtual[:, None] + virtual[None, :] - occupied
            residual = integral + denominator * own - coupled
            return own - residual / denominator

        current = lax.map(update, (couplings, fock_coupling, intersections, integrals, virt_energy, occ_pair_energy, current))
    return current
```

```python
import functools

import jax
import jax.numpy as jnp
from jax import lax
from jax.experimental import pallas as pl
from jax.experimental.pallas import tpu as pltpu
from jax.sharding import PartitionSpec as P

MESH = pl.DeviceIdType.MESH
F32 = jnp.float32
BF16 = jnp.bfloat16
NT = (((1,), (1,)), ((), ()))

CUT = 256

IDX_P, IDX_X = 0, 1
SLAB_P = 2
SLAB_A = 4
SLAB_B = 6
SLAB_F = 8
AMP_P = 10
AMP_X = 12
CUR_P = 14
CUR_X = 16
KINDS = 18

OWN, PARTNER, FORWARDED, ACROSS, ACROSS2 = 0, 2, 4, 6, 8


def split(x):
    high = x.astype(BF16)
    return high, (x - high.astype(F32)).astype(BF16)


def dot_nn(a, b):
    return jnp.dot(a, b, preferred_element_type=F32)


def dot_nt(a, b):
    return lax.dot_general(a, b, NT, preferred_element_type=F32)


def transform(gain, full, chunk, first):
    width = chunk.shape[1]
    full_hi, full_lo = split(full)
    chunk_hi, chunk_lo = split(chunk)
    half = gain * dot_nn(
        jnp.concatenate([full_hi, full_hi, full_lo], axis=1),
        jnp.concatenate([chunk_hi, chunk_lo, chunk_hi], axis=0),
    )
    half_hi, half_lo = split(half)
    part_hi = full_hi[:, first : first + width]
    part_lo = full_lo[:, first : first + width]
    return dot_nt(
        jnp.concatenate([half_hi, half_hi, half_lo], axis=1),
        jnp.concatenate([part_hi, part_lo, part_hi], axis=1),
    )


def slab_product(left, right):
    left_hi, left_lo = split(left)
    right_hi, right_lo = split(right)
    return dot_nt(left_hi, right_hi) + dot_nt(left_hi, right_lo) + dot_nt(left_lo, right_hi)


def kernel(
    devices,
    couplings,
    pair_orbs,
    fock,
    occupied,
    virtual,
    slabs,
    amplitudes,
    intersections,
    out,
    cur,
    acc0,
    acc1,
    inter_own,
    inter_p,
    inter_x,
    left,
    win0,
    win1,
    amp_p0,
    amp_p1,
    amp_x0,
    amp_x1,
    cur_p0,
    cur_p1,
    cur_x0,
    cur_x1,
    out_p0,
    out_p1,
    out_x0,
    out_x1,
    idx_p,
    idx_x,
    pick,
    slot,
    send_sem,
    recv_sem,
    local_sem,
    store_sem,
):
    pairs, nv = cur.shape[0], cur.shape[1]
    picks = out_p0.shape[0]
    orbitals = left.shape[0]
    me = lax.axis_index("orb")
    side = 1 - 2 * lax.rem(me, 2)
    partner = me + side
    across = lax.rem(me - side + devices, devices)
    target2 = lax.rem(me + 2 * side + devices, devices)
    source2 = lax.rem(me - 2 * side + devices, devices)
    column_p = lax.rem(me + 1, 2)
    column_x = lax.rem(me, 2)

    local = []

    def fetch(src, dst):
        copy = pltpu.make_async_copy(src, dst, local_sem.at[len(local)])
        local.append(copy)
        copy.start()
        return copy

    get_cur = fetch(amplitudes, cur)
    get_own = fetch(intersections.at[:, 2], inter_own)
    get_p = fetch(intersections.at[:, column_p], inter_p)
    get_left = fetch(slabs, left)
    get_win0 = fetch(slabs.at[:, pl.ds(0, CUT)], win0.at[pl.ds(OWN, orbitals)])
    get_win1 = fetch(slabs.at[:, pl.ds(CUT, nv - CUT)], win1.at[pl.ds(OWN, orbitals)])
    get_x = fetch(intersections.at[:, column_x], inter_x)

    barrier = pltpu.get_barrier_semaphore()
    for other in (partner, across, target2, source2):
        pl.semaphore_signal(barrier, inc=1, device_id=(other,), device_id_type=MESH)
    pl.semaphore_wait(barrier, 4)

    def remote(src, dst, kind, device):
        return pltpu.make_async_remote_copy(
            src_ref=src,
            dst_ref=dst,
            send_sem=send_sem.at[kind],
            recv_sem=recv_sem.at[kind],
            device_id=(device,),
            device_id_type=MESH,
        )

    slab0 = slabs.at[:, pl.ds(0, CUT)]
    slab1 = slabs.at[:, pl.ds(CUT, nv - CUT)]
    rows = lambda first: pl.ds(first, orbitals)
    send_idx_p = remote(couplings, idx_p, IDX_P, partner)
    send_idx_x = remote(couplings, idx_x, IDX_X, across)
    send_p0 = remote(slab0, win0.at[rows(PARTNER)], SLAB_P, partner)
    send_p1 = remote(slab1, win1.at[rows(PARTNER)], SLAB_P + 1, partner)
    send_a0 = remote(slab0, win0.at[rows(ACROSS)], SLAB_A, across)
    send_a1 = remote(slab1, win1.at[rows(ACROSS)], SLAB_A + 1, across)
    send_b0 = remote(slab0, win0.at[rows(ACROSS2)], SLAB_B, target2)
    send_b1 = remote(slab1, win1.at[rows(ACROSS2)], SLAB_B + 1, target2)
    send_f0 = remote(win0.at[rows(ACROSS)], win0.at[rows(FORWARDED)], SLAB_F, partner)
    send_f1 = remote(win1.at[rows(ACROSS)], win1.at[rows(FORWARDED)], SLAB_F + 1, partner)
    send_amp_p0 = remote(out_p0, amp_p0, AMP_P, partner)
    send_amp_p1 = remote(out_p1, amp_p1, AMP_P + 1, partner)
    send_amp_x0 = remote(out_x0, amp_x0, AMP_X, across)
    send_amp_x1 = remote(out_x1, amp_x1, AMP_X + 1, across)
    send_cur_p0 = remote(out_p0, cur_p0, CUR_P, partner)
    send_cur_p1 = remote(out_p1, cur_p1, CUR_P + 1, partner)
    send_cur_x0 = remote(out_x0, cur_x0, CUR_X, across)
    send_cur_x1 = remote(out_x1, cur_x1, CUR_X + 1, across)

    send_idx_x.start()
    send_idx_p.start()
    send_a0.start()
    send_b0.start()
    send_b1.start()
    send_p0.start()
    send_p1.start()

    def tables(source, column, base):
        named = [source[p, column] - base for p in range(pairs)]
        present = []
        for q in range(pairs):
            hit = jnp.int32(0)
            for value in named:
                hit = jnp.maximum(hit, (value == q).astype(jnp.int32))
            present.append(hit)
        below = [jnp.int32(0)]
        for q in range(pairs - 1):
            below.append(below[-1] + present[q])
        return named, present, below

    for row, column, owner in ((0, column_p, partner), (1, column_x, across)):
        named, present, below = tables(couplings, column, owner * pairs)
        for p in range(pairs):
            value = jnp.int32(0)
            for q in range(pairs):
                value = value + jnp.where(named[p] == q, below[q], 0)
            slot[row, p] = jnp.minimum(value, picks - 1)

    send_idx_x.wait_recv()
    send_idx_p.wait_recv()
    for row, column, source in ((0, column_x, idx_p), (1, column_p, idx_x)):
        _, present, below = tables(source, column, me * pairs)
        for s in range(picks):
            value = jnp.int32(0)
            for q in range(pairs):
                chosen = jnp.logical_and(present[q] == 1, below[q] == s)
                value = value + jnp.where(chosen, q, 0)
            pick[row, s] = jnp.minimum(value, pairs - 1)

    def gather(row, dst, first):
        width = dst.shape[2]

        def step(s, carry):
            dst[s] = cur[pick[row, s], :, first : first + width]
            return carry

        lax.fori_loop(0, picks, step, 0)

    get_cur.wait()
    gather(1, out_x0, 0)
    gather(1, out_x1, CUT)
    send_amp_x0.start()
    send_amp_x1.start()
    send_a1.start()
    gather(0, out_p0, 0)
    gather(0, out_p1, CUT)
    send_amp_p0.start()
    send_amp_p1.start()

    def each_pair(step):
        def body(p, carry):
            step(p)
            return carry

        lax.fori_loop(0, pairs, body, 0)

    def third(p):
        return jnp.clip(couplings[p, 2] - me * pairs, 0, pairs - 1)

    get_own.wait()

    def own_first(p):
        chosen = cur[third(p)]
        acc0[p] = transform(fock[p, 2], inter_own[p], chosen, 0)

    each_pair(own_first)

    get_p.wait()
    send_amp_p0.wait_recv()
    send_amp_p1.wait_recv()

    def partner_first(p):
        q = slot[0, p]
        chosen = jnp.concatenate([amp_p0[q], amp_p1[q]], axis=1)
        acc0[p] += transform(fock[p, column_p], inter_p[p], chosen, 0)

    each_pair(partner_first)

    def second(p):
        offset = lax.div(pair_orbs[p, 1], orbitals) - me
        parity = lax.rem(pair_orbs[p, 1], orbitals)
        turned = offset * side
        place = jnp.where(turned >= 0, turned, 2 - turned)
        return jnp.clip(place * orbitals + parity, 0, win0.shape[0] - 1)

    def first_of(p):
        return jnp.clip(pair_orbs[p, 0] - me * orbitals, 0, orbitals - 1)

    send_a0.wait_recv()
    send_f0.start()
    get_left.wait()
    get_win0.wait()
    send_p0.wait_recv()
    send_b0.wait_recv()
    send_f0.wait_recv()

    def integrals0(p):
        acc1[p, :, 0:CUT] = -slab_product(left[first_of(p)], win0[second(p)])

    each_pair(integrals0)

    get_x.wait()
    send_amp_x0.wait_recv()
    send_amp_x1.wait_recv()

    def across_first(p):
        q = slot[1, p]
        chosen = jnp.concatenate([amp_x0[q], amp_x1[q]], axis=1)
        acc0[p] += transform(fock[p, column_x], inter_x[p], chosen, 0)

    each_pair(across_first)

    def denominator(p, first, width):
        row = virtual[pl.ds(p, 1), :]
        column = jnp.broadcast_to(row, (128, nv)).T
        if width > 128:
            column = jnp.concatenate([column] * (width // 128), axis=1)
        return column + row[:, first : first + width] - occupied[p]

    def update0(p):
        denom = denominator(p, 0, CUT)
        old = cur[p, :, 0:CUT]
        residual = denom * old - acc1[p, :, 0:CUT] - acc0[p, :, 0:CUT]
        cur[p, :, 0:CUT] = old - residual / denom

    each_pair(update0)

    send_amp_x0.wait_send()
    send_amp_x1.wait_send()
    send_amp_p0.wait_send()
    send_amp_p1.wait_send()
    gather(1, out_x0, 0)
    send_cur_x0.start()
    gather(0, out_p0, 0)
    send_cur_p0.start()

    def own_second0(p):
        chosen = cur[third(p), :, 0:CUT]
        whole = transform(fock[p, 2], inter_own[p], chosen, 0)
        acc1[p, :, 0:CUT] += whole[:, 0:CUT]
        acc1[p, :, CUT:nv] = whole[:, CUT:nv]

    each_pair(own_second0)

    send_a1.wait_recv()
    send_f1.start()
    send_cur_p0.wait_recv()

    def partner_second0(p):
        acc1[p] += transform(fock[p, column_p], inter_p[p], cur_p0[slot[0, p]], 0)

    each_pair(partner_second0)

    get_win1.wait()
    send_p1.wait_recv()
    send_b1.wait_recv()
    send_f1.wait_recv()

    def update1(p):
        product = slab_product(left[first_of(p)], win1[second(p)])
        denom = denominator(p, CUT, nv - CUT)
        old = cur[p, :, CUT:nv]
        residual = product + denom * old - acc0[p, :, CUT:nv]
        cur[p, :, CUT:nv] = old - residual / denom
        acc1[p, :, CUT:nv] -= product

    each_pair(update1)

    gather(1, out_x1, CUT)
    send_cur_x1.start()
    gather(0, out_p1, CUT)
    send_cur_p1.start()

    def own_second1(p):
        chosen = cur[third(p), :, CUT:nv]
        acc1[p] += transform(fock[p, 2], inter_own[p], chosen, CUT)

    each_pair(own_second1)

    send_cur_p1.wait_recv()

    def partner_second1(p):
        acc1[p] += transform(fock[p, column_p], inter_p[p], cur_p1[slot[0, p]], CUT)

    each_pair(partner_second1)

    send_cur_x0.wait_recv()

    def across_second0(p):
        acc1[p] += transform(fock[p, column_x], inter_x[p], cur_x0[slot[1, p]], 0)

    each_pair(across_second0)

    send_cur_x1.wait_recv()

    def store(p):
        return pltpu.make_async_copy(cur.at[p], out.at[p], store_sem.at[p])

    def across_second1(p):
        whole = acc1[p] + transform(fock[p, column_x], inter_x[p], cur_x1[slot[1, p]], CUT)
        denom = denominator(p, 0, nv)
        old = cur[p]
        cur[p] = old - (denom * old - whole) / denom
        store(p).start()

    each_pair(across_second1)

    for copy in (
        send_idx_p,
        send_idx_x,
        send_p0,
        send_p1,
        send_a0,
        send_a1,
        send_b0,
        send_b1,
        send_f0,
        send_f1,
        send_cur_p0,
        send_cur_p1,
        send_cur_x0,
        send_cur_x1,
    ):
        copy.wait_send()
    each_pair(lambda p: store(p).wait())


def shards(
    slabs,
    amplitudes,
    intersections,
    fock_coupling,
    virt_energy,
    occ_pair_energy,
    pair_orbs,
    couplings,
):
    devices = lax.axis_size("orb")
    orbitals, nv, nq = slabs.shape
    pairs = amplitudes.shape[0]
    picks = pairs // 2
    smem = pl.BlockSpec(memory_space=pltpu.SMEM)
    vmem = pl.BlockSpec(memory_space=pltpu.VMEM)
    hbm = pl.BlockSpec(memory_space=pl.ANY)
    block = lambda count, width: pltpu.VMEM((count, nv, width), F32)
    pieces = [block(picks, CUT), block(picks, nv - CUT)]
    return pl.pallas_call(
        functools.partial(kernel, devices),
        out_shape=jax.ShapeDtypeStruct(amplitudes.shape, F32),
        in_specs=[smem, smem, smem, smem, vmem, hbm, hbm, hbm],
        out_specs=hbm,
        scratch_shapes=[
            block(pairs, nv),
            block(pairs, nv),
            block(pairs, nv),
            block(pairs, nv),
            block(pairs, nv),
            block(pairs, nv),
            block(orbitals, nq),
            pltpu.VMEM((5 * orbitals, CUT, nq), F32),
            pltpu.VMEM((5 * orbitals, nv - CUT, nq), F32),
            *(pieces * 6),
            pltpu.SMEM(couplings.shape, jnp.int32),
            pltpu.SMEM(couplings.shape, jnp.int32),
            pltpu.SMEM((2, picks), jnp.int32),
            pltpu.SMEM((2, pairs), jnp.int32),
            pltpu.SemaphoreType.DMA((KINDS,)),
            pltpu.SemaphoreType.DMA((KINDS,)),
            pltpu.SemaphoreType.DMA((7,)),
            pltpu.SemaphoreType.DMA((pairs,)),
        ],
        compiler_params=pltpu.CompilerParams(
            collective_id=0, has_side_effects=True, vmem_limit_bytes=67043328
        ),
        name="amplitudes",
    )(
        couplings,
        pair_orbs,
        fock_coupling,
        occ_pair_energy,
        virt_energy,
        slabs,
        amplitudes,
        intersections,
    )


def solution(mesh):
    in_specs = (
        P("orb", None, None),
        P("orb", None, None),
        P("orb", None, None, None),
        P("orb", None),
        P("orb", None),
        P("orb"),
        P("orb", None),
        P("orb", None),
    )
    out_specs = P("orb", None, None)
    return jax.shard_map(shards, mesh=mesh, in_specs=in_specs, out_specs=out_specs, check_vma=False)
```

```python
import functools

import jax
import jax.numpy as jnp
from jax import lax
from jax.experimental import pallas as pl
from jax.experimental.pallas import tpu as pltpu
from jax.sharding import PartitionSpec as P

MESH = pl.DeviceIdType.MESH
F32 = jnp.float32
BF16 = jnp.bfloat16
NT = (((1,), (1,)), ((), ()))

CUT = 256

PER_TURN = 2

IDX_P, IDX_X = 0, 1
SLAB_P = 2
SLAB_A = 4
SLAB_B = 6
SLAB_F = 8
AMP_P = 10
AMP_X = 12
CUR_P = 14
CUR_X = 16
KINDS = 18

OWN, PARTNER, FORWARDED, ACROSS, ACROSS2 = 0, 2, 4, 6, 8


def split(x):
    high = x.astype(BF16)
    return high, (x - high.astype(F32)).astype(BF16)


def dot_nn(a, b):
    return jnp.dot(a, b, preferred_element_type=F32)


def dot_nt(a, b):
    return lax.dot_general(a, b, NT, preferred_element_type=F32)


def by_halves(dot, a, b):
    middle = a.shape[0] // 2
    return jnp.concatenate([dot(a[:middle], b), dot(a[middle:], b)], axis=0)


def transform(gain, full, chunk, first):
    width = chunk.shape[1]
    full_hi, full_lo = split(full)
    chunk_hi, chunk_lo = split(gain * chunk)
    half = by_halves(
        dot_nn,
        jnp.concatenate([full_hi, full_hi, full_lo], axis=1),
        jnp.concatenate([chunk_hi, chunk_lo, chunk_hi], axis=0),
    )
    half_hi, half_lo = split(half)
    part_hi = full_hi[:, first : first + width]
    part_lo = full_lo[:, first : first + width]
    return dot_nt(
        jnp.concatenate([half_hi, half_hi, half_lo], axis=1),
        jnp.concatenate([part_hi, part_lo, part_hi], axis=1),
    )


def slab_product(left, right):
    left_hi, left_lo = split(left)
    right_hi, right_lo = split(right)
    return by_halves(
        dot_nt,
        jnp.concatenate([left_hi, left_hi, left_lo], axis=1),
        jnp.concatenate([right_hi, right_lo, right_hi], axis=1),
    )


def kernel(
    devices,
    couplings,
    pair_orbs,
    fock,
    occupied,
    virtual,
    slabs,
    amplitudes,
    intersections,
    cur,
    acc0,
    acc1,
    inter_own,
    inter_p,
    inter_x,
    left,
    win0,
    win1,
    amp_p0,
    amp_p1,
    amp_x0,
    amp_x1,
    cur_p0,
    cur_p1,
    cur_x0,
    cur_x1,
    out_p0,
    out_p1,
    out_x0,
    out_x1,
    idx_p,
    idx_x,
    pick,
    slot,
    send_sem,
    recv_sem,
    local_sem,
):
    pairs, nv = cur.shape[0], cur.shape[1]
    picks = out_p0.shape[0]
    orbitals = left.shape[0]
    me = lax.axis_index("orb")
    side = 1 - 2 * lax.rem(me, 2)
    partner = me + side
    across = lax.rem(me - side + devices, devices)
    target2 = lax.rem(me + 2 * side + devices, devices)
    source2 = lax.rem(me - 2 * side + devices, devices)
    column_p = lax.rem(me + 1, 2)
    column_x = lax.rem(me, 2)

    local = []

    def fetch(src, dst):
        copy = pltpu.make_async_copy(src, dst, local_sem.at[len(local)])
        local.append(copy)
        copy.start()
        return copy

    get_cur = fetch(amplitudes, cur)
    get_own = fetch(intersections.at[:, 2], inter_own)
    get_p = fetch(intersections.at[:, column_p], inter_p)
    get_left = fetch(slabs, left)
    get_win0 = fetch(slabs.at[:, pl.ds(0, CUT)], win0.at[pl.ds(OWN, orbitals)])
    get_win1 = fetch(slabs.at[:, pl.ds(CUT, nv - CUT)], win1.at[pl.ds(OWN, orbitals)])
    get_x = fetch(intersections.at[:, column_x], inter_x)

    barrier = pltpu.get_barrier_semaphore()
    for other in (partner, across, target2, source2):
        pl.semaphore_signal(barrier, inc=1, device_id=(other,), device_id_type=MESH)
    pl.semaphore_wait(barrier, 4)

    def remote(src, dst, kind, device):
        return pltpu.make_async_remote_copy(
            src_ref=src,
            dst_ref=dst,
            send_sem=send_sem.at[kind],
            recv_sem=recv_sem.at[kind],
            device_id=(device,),
            device_id_type=MESH,
        )

    slab0 = slabs.at[:, pl.ds(0, CUT)]
    slab1 = slabs.at[:, pl.ds(CUT, nv - CUT)]
    rows = lambda first: pl.ds(first, orbitals)
    send_idx_p = remote(couplings, idx_p, IDX_P, partner)
    send_idx_x = remote(couplings, idx_x, IDX_X, across)
    send_p0 = remote(slab0, win0.at[rows(PARTNER)], SLAB_P, partner)
    send_p1 = remote(slab1, win1.at[rows(PARTNER)], SLAB_P + 1, partner)
    send_a0 = remote(slab0, win0.at[rows(ACROSS)], SLAB_A, across)
    send_a1 = remote(slab1, win1.at[rows(ACROSS)], SLAB_A + 1, across)
    send_b0 = remote(slab0, win0.at[rows(ACROSS2)], SLAB_B, target2)
    send_b1 = remote(slab1, win1.at[rows(ACROSS2)], SLAB_B + 1, target2)
    send_f0 = remote(win0.at[rows(ACROSS)], win0.at[rows(FORWARDED)], SLAB_F, partner)
    send_f1 = remote(win1.at[rows(ACROSS)], win1.at[rows(FORWARDED)], SLAB_F + 1, partner)
    send_amp_p0 = remote(out_p0, amp_p0, AMP_P, partner)
    send_amp_p1 = remote(out_p1, amp_p1, AMP_P + 1, partner)
    send_amp_x0 = remote(out_x0, amp_x0, AMP_X, across)
    send_amp_x1 = remote(out_x1, amp_x1, AMP_X + 1, across)
    send_cur_p0 = remote(out_p0, cur_p0, CUR_P, partner)
    send_cur_p1 = remote(out_p1, cur_p1, CUR_P + 1, partner)
    send_cur_x0 = remote(out_x0, cur_x0, CUR_X, across)
    send_cur_x1 = remote(out_x1, cur_x1, CUR_X + 1, across)

    send_idx_x.start()
    send_idx_p.start()
    send_a0.start()
    send_b0.start()
    send_p0.start()
    send_p1.start()

    def tables(source, column, base):
        named = [source[column, p] - base for p in range(pairs)]
        present = []
        for q in range(pairs):
            hit = jnp.int32(0)
            for value in named:
                hit = jnp.maximum(hit, (value == q).astype(jnp.int32))
            present.append(hit)
        below = [jnp.int32(0)]
        for q in range(pairs - 1):
            below.append(below[-1] + present[q])
        return named, present, below

    for row, column, owner in ((0, column_p, partner), (1, column_x, across)):
        named, present, below = tables(couplings, column, owner * pairs)
        for p in range(pairs):
            value = jnp.int32(0)
            for q in range(pairs):
                value = value + jnp.where(named[p] == q, below[q], 0)
            slot[row, p] = jnp.minimum(value, picks - 1)

    send_idx_x.wait_recv()
    send_idx_p.wait_recv()
    for row, column, source in ((0, column_x, idx_p), (1, column_p, idx_x)):
        _, present, below = tables(source, column, me * pairs)
        for s in range(picks):
            value = jnp.int32(0)
            for q in range(pairs):
                chosen = jnp.logical_and(present[q] == 1, below[q] == s)
                value = value + jnp.where(chosen, q, 0)
            pick[row, s] = jnp.minimum(value, pairs - 1)

    def gather(row, dst, first):
        width = dst.shape[2]

        def step(s, carry):
            dst[s] = cur[pick[row, s], :, first : first + width]
            return carry

        lax.fori_loop(0, picks, step, 0)

    get_cur.wait()
    gather(1, out_x0, 0)
    gather(1, out_x1, CUT)
    send_amp_x0.start()
    send_amp_x1.start()
    send_a1.start()
    gather(0, out_p0, 0)
    gather(0, out_p1, CUT)
    send_amp_p0.start()
    send_amp_p1.start()

    def each_pair(step):
        def body(turn, carry):
            for p in range(PER_TURN):
                step(turn * PER_TURN + p)
            return carry

        lax.fori_loop(0, pairs // PER_TURN, body, 0)

    def third(p):
        return jnp.clip(couplings[2, p] - me * pairs, 0, pairs - 1)

    get_own.wait()

    def own_first(p):
        chosen = cur[third(p)]
        acc0[p] = transform(fock[2, p], inter_own[p], chosen, 0)

    each_pair(own_first)

    get_p.wait()
    send_amp_p0.wait_recv()
    send_amp_p1.wait_recv()

    def partner_first(p):
        q = slot[0, p]
        chosen = jnp.concatenate([amp_p0[q], amp_p1[q]], axis=1)
        acc0[p] += transform(fock[column_p, p], inter_p[p], chosen, 0)

    each_pair(partner_first)

    def second(p):
        offset = lax.div(pair_orbs[1, p], orbitals) - me
        parity = lax.rem(pair_orbs[1, p], orbitals)
        turned = offset * side
        place = jnp.where(turned >= 0, turned, 2 - turned)
        return jnp.clip(place * orbitals + parity, 0, win0.shape[0] - 1)

    def first_of(p):
        return jnp.clip(pair_orbs[0, p] - me * orbitals, 0, orbitals - 1)

    send_a0.wait_recv()
    send_f0.start()
    get_left.wait()
    get_win0.wait()
    send_p0.wait_recv()
    send_b0.wait_recv()
    send_f0.wait_recv()

    def integrals0(p):
        acc1[p, :, 0:CUT] = -slab_product(left[first_of(p)], win0[second(p)])

    each_pair(integrals0)

    get_x.wait()
    send_amp_x0.wait_recv()

    def across_first0(p):
        acc0[p] += transform(fock[column_x, p], inter_x[p], amp_x0[slot[1, p]], 0)

    each_pair(across_first0)

    send_amp_x1.wait_recv()
    send_b1.start()

    def across_first1(p):
        acc0[p] += transform(fock[column_x, p], inter_x[p], amp_x1[slot[1, p]], CUT)

    each_pair(across_first1)

    def denominator(p, first, width):
        row = virtual[pl.ds(p, 1), :]
        column = jnp.broadcast_to(row, (128, nv)).T
        if width > 128:
            column = jnp.concatenate([column] * (width // 128), axis=1)
        return column + row[:, first : first + width] - occupied[p]

    def update0(p):
        denom = denominator(p, 0, CUT)
        old = cur[p, :, 0:CUT]
        residual = denom * old - acc1[p, :, 0:CUT] - acc0[p, :, 0:CUT]
        cur[p, :, 0:CUT] = old - residual / denom

    each_pair(update0)

    send_amp_x0.wait_send()
    send_amp_x1.wait_send()
    send_amp_p0.wait_send()
    send_amp_p1.wait_send()
    gather(1, out_x0, 0)
    send_cur_x0.start()
    gather(0, out_p0, 0)
    send_cur_p0.start()

    def own_second0(p):
        chosen = cur[third(p), :, 0:CUT]
        whole = transform(fock[2, p], inter_own[p], chosen, 0)
        acc1[p, :, 0:CUT] += whole[:, 0:CUT]
        acc1[p, :, CUT:nv] = whole[:, CUT:nv]

    each_pair(own_second0)

    send_a1.wait_recv()
    send_f1.start()
    send_cur_p0.wait_recv()

    def partner_second0(p):
        acc1[p] += transform(fock[column_p, p], inter_p[p], cur_p0[slot[0, p]], 0)

    each_pair(partner_second0)

    get_win1.wait()
    send_p1.wait_recv()
    send_b1.wait_recv()
    send_f1.wait_recv()

    def update1(p):
        product = slab_product(left[first_of(p)], win1[second(p)])
        denom = denominator(p, CUT, nv - CUT)
        old = cur[p, :, CUT:nv]
        residual = product + denom * old - acc0[p, :, CUT:nv]
        cur[p, :, CUT:nv] = old - residual / denom
        acc1[p, :, CUT:nv] -= product

    each_pair(update1)

    gather(1, out_x1, CUT)
    send_cur_x1.start()
    gather(0, out_p1, CUT)
    send_cur_p1.start()

    def own_second1(p):
        chosen = cur[third(p), :, CUT:nv]
        acc1[p] += transform(fock[2, p], inter_own[p], chosen, CUT)

    each_pair(own_second1)

    send_cur_p1.wait_recv()

    def partner_second1(p):
        acc1[p] += transform(fock[column_p, p], inter_p[p], cur_p1[slot[0, p]], CUT)

    each_pair(partner_second1)

    send_cur_x0.wait_recv()

    def across_second0(p):
        acc1[p] += transform(fock[column_x, p], inter_x[p], cur_x0[slot[1, p]], 0)

    each_pair(across_second0)

    send_cur_x1.wait_recv()

    def across_second1(p):
        whole = acc1[p] + transform(fock[column_x, p], inter_x[p], cur_x1[slot[1, p]], CUT)
        denom = denominator(p, 0, nv)
        old = cur[p]
        cur[p] = old - (denom * old - whole) / denom

    each_pair(across_second1)

    for copy in (
        send_idx_p,
        send_idx_x,
        send_p0,
        send_p1,
        send_a0,
        send_a1,
        send_b0,
        send_b1,
        send_f0,
        send_f1,
        send_cur_p0,
        send_cur_p1,
        send_cur_x0,
        send_cur_x1,
    ):
        copy.wait_send()


def shards(
    slabs,
    amplitudes,
    intersections,
    fock_coupling,
    virt_energy,
    occ_pair_energy,
    pair_orbs,
    couplings,
):
    devices = lax.axis_size("orb")
    orbitals, nv, nq = slabs.shape
    pairs = amplitudes.shape[0]
    picks = pairs // 2
    smem = pl.BlockSpec(memory_space=pltpu.SMEM)
    vmem = pl.BlockSpec(memory_space=pltpu.VMEM)
    hbm = pl.BlockSpec(memory_space=pl.ANY)
    block = lambda count, width: pltpu.VMEM((count, nv, width), F32)
    pieces = [block(picks, CUT), block(picks, nv - CUT)]
    return pl.pallas_call(
        functools.partial(kernel, devices),
        out_shape=pltpu.VMEM(amplitudes.shape, F32),
        in_specs=[smem, smem, smem, smem, vmem, hbm, hbm, hbm],
        out_specs=vmem,
        scratch_shapes=[
            block(pairs, nv),
            block(pairs, nv),
            block(pairs, nv),
            block(pairs, nv),
            block(pairs, nv),
            block(orbitals, nq),
            pltpu.VMEM((5 * orbitals, CUT, nq), F32),
            pltpu.VMEM((5 * orbitals, nv - CUT, nq), F32),
            *(pieces * 6),
            pltpu.SMEM(couplings.shape[::-1], jnp.int32),
            pltpu.SMEM(couplings.shape[::-1], jnp.int32),
            pltpu.SMEM((2, picks), jnp.int32),
            pltpu.SMEM((2, pairs), jnp.int32),
            pltpu.SemaphoreType.DMA((KINDS,)),
            pltpu.SemaphoreType.DMA((KINDS,)),
            pltpu.SemaphoreType.DMA((7,)),
        ],
        compiler_params=pltpu.CompilerParams(
            collective_id=0, has_side_effects=True, vmem_limit_bytes=62000000
        ),
        name="amplitudes",
    )(
        couplings.T,
        pair_orbs.T,
        fock_coupling.T,
        occ_pair_energy,
        virt_energy,
        slabs,
        amplitudes,
        intersections,
    )


def solution(mesh):
    in_specs = (
        P("orb", None, None),
        P("orb", None, None),
        P("orb", None, None, None),
        P("orb", None),
        P("orb", None),
        P("orb"),
        P("orb", None),
        P("orb", None),
    )
    out_specs = P("orb", None, None)
    return jax.shard_map(shards, mesh=mesh, in_specs=in_specs, out_specs=out_specs, check_vma=False)
```

```python
import functools

import jax
import jax.numpy as jnp
from jax import lax
from jax.experimental import pallas as pl
from jax.experimental.pallas import tpu as pltpu
from jax.sharding import PartitionSpec as P

MESH = pl.DeviceIdType.MESH
F32 = jnp.float32
BF16 = jnp.bfloat16
NT = (((1,), (1,)), ((), ()))

CUT = 256

PER_TURN = 4

IDX_P, IDX_X = 0, 1
SLAB_P = 2
SLAB_A = 4
SLAB_B = 6
SLAB_F = 8
AMP_P = 10
AMP_X = 12
CUR_P = 14
CUR_X = 16
CUR_X_LAST = 18
KINDS = 19

OWN, PARTNER, FORWARDED, ACROSS, ACROSS2 = 0, 2, 4, 6, 8


def split(x):
    high = x.astype(BF16)
    return high, (x - high.astype(F32)).astype(BF16)


def dot_nn(a, b):
    return jnp.dot(a, b, preferred_element_type=F32)


def dot_nt(a, b):
    return lax.dot_general(a, b, NT, preferred_element_type=F32)


def by_halves(dot, a, b):
    middle = a.shape[0] // 2
    return jnp.concatenate([dot(a[:middle], b), dot(a[middle:], b)], axis=0)


def wide_half(full_hi, full_lo, chunk_hi, chunk_lo):
    return by_halves(
        dot_nn,
        jnp.concatenate([full_hi, full_hi, full_lo], axis=1),
        jnp.concatenate([chunk_hi, chunk_lo, chunk_hi], axis=0),
    )


def folded(product):
    width = product.shape[1] // 2
    return product[:, :width] + product[:, width:]


def narrow_half_upper(full_hi, full_lo, chunk_hi, chunk_lo):
    both = by_halves(dot_nn, full_hi, jnp.concatenate([chunk_hi, chunk_lo], axis=1))
    return folded(both) + by_halves(dot_nn, full_lo, chunk_hi)


def narrow_half_lower(full_hi, full_lo, chunk_hi, chunk_lo):
    upper = jnp.concatenate([chunk_hi, chunk_lo], axis=1)
    lower = jnp.concatenate([chunk_hi, jnp.zeros_like(chunk_lo)], axis=1)
    return folded(
        by_halves(
            dot_nn,
            jnp.concatenate([full_hi, full_lo], axis=1),
            jnp.concatenate([upper, lower], axis=0),
        )
    )


def second_product(half, part_hi, part_lo):
    half_hi, half_lo = split(half)
    return by_halves(
        dot_nt,
        jnp.concatenate([half_hi, half_hi, half_lo], axis=1),
        jnp.concatenate([part_hi, part_lo, part_hi], axis=1),
    )


def transform(gain, full, chunk, first):
    width = chunk.shape[1]
    full_hi, full_lo = split(full)
    chunk_hi, chunk_lo = split(gain * chunk)
    if width > 128:
        half = wide_half(full_hi, full_lo, chunk_hi, chunk_lo)
    else:
        half = narrow_half_upper(
            full_hi[:, :CUT], full_lo[:, :CUT], chunk_hi[:CUT], chunk_lo[:CUT]
        ) + narrow_half_lower(full_hi[:, CUT:], full_lo[:, CUT:], chunk_hi[CUT:], chunk_lo[CUT:])
    return second_product(
        half, full_hi[:, first : first + width], full_lo[:, first : first + width]
    )


def slab_product(left, right):
    left_hi, left_lo = split(left)
    right_hi, right_lo = split(right)
    return by_halves(
        dot_nt,
        jnp.concatenate([left_hi, left_hi, left_lo], axis=1),
        jnp.concatenate([right_hi, right_lo, right_hi], axis=1),
    )


def kernel(
    devices,
    couplings,
    pair_orbs,
    fock,
    occupied,
    virtual,
    slabs,
    amplitudes,
    intersections,
    cur,
    acc0,
    acc1,
    inter_own,
    inter_p,
    inter_x,
    left,
    win0,
    win1,
    amp_p0,
    amp_p1,
    amp_x0,
    amp_x1,
    cur_p0,
    cur_p1,
    cur_x0,
    cur_x1a,
    cur_x1b,
    out_p0,
    out_p1,
    out_x0,
    out_x1,
    idx_p,
    idx_x,
    pick,
    slot,
    halves,
    send_sem,
    recv_sem,
    local_sem,
    fill_sem,
):
    pairs, nv = cur.shape[0], cur.shape[1]
    picks = out_p0.shape[0]
    orbitals = left.shape[0]
    me = lax.axis_index("orb")
    side = 1 - 2 * lax.rem(me, 2)
    partner = me + side
    across = lax.rem(me - side + devices, devices)
    target2 = lax.rem(me + 2 * side + devices, devices)
    source2 = lax.rem(me - 2 * side + devices, devices)
    column_p = lax.rem(me + 1, 2)
    column_x = lax.rem(me, 2)

    local = []

    def fetch(src, dst):
        copy = pltpu.make_async_copy(src, dst, local_sem.at[len(local)])
        local.append(copy)
        copy.start()
        return copy

    get_cur = fetch(amplitudes, cur)
    get_own = fetch(intersections.at[:, 2], inter_own)
    get_p = fetch(intersections.at[:, column_p], inter_p)
    get_left = fetch(slabs, left)
    get_win0 = fetch(slabs.at[:, pl.ds(0, CUT)], win0.at[pl.ds(OWN, orbitals)])
    get_win1 = fetch(slabs.at[:, pl.ds(CUT, nv - CUT)], win1.at[pl.ds(OWN, orbitals)])
    get_x = fetch(intersections.at[:, column_x], inter_x)

    sends_across = jnp.logical_and(me != devices - 1, me != 0)
    sends_two_across = jnp.logical_and(me != devices - 2, me != 1)
    gets_across = jnp.logical_and(me != 0, me != devices - 1)
    gets_forwarded = jnp.logical_and(me != 1, me != devices - 2)

    def choose(found, then, otherwise=None):
        pl.when(found)(then)
        if otherwise is not None:
            pl.when(jnp.logical_not(found))(otherwise)

    barrier = pltpu.get_barrier_semaphore()

    def greet(other):
        pl.semaphore_signal(barrier, inc=1, device_id=(other,), device_id_type=MESH)

    greet(partner)
    greet(across)
    choose(sends_two_across, lambda: greet(target2))
    choose(gets_across, lambda: greet(source2))
    greeted = 2 + sends_two_across.astype(jnp.int32) + gets_across.astype(jnp.int32)
    pl.semaphore_wait(barrier, greeted)

    def remote(src, dst, kind, device):
        return pltpu.make_async_remote_copy(
            src_ref=src,
            dst_ref=dst,
            send_sem=send_sem.at[kind],
            recv_sem=recv_sem.at[kind],
            device_id=(device,),
            device_id_type=MESH,
        )

    slab0 = slabs.at[:, pl.ds(0, CUT)]
    slab1 = slabs.at[:, pl.ds(CUT, nv - CUT)]
    rows = lambda first: pl.ds(first, orbitals)
    def fill(src, window, *places):
        for place in places:
            copy = pltpu.make_async_copy(src, window.at[rows(place)], fill_sem)
            copy.start()
            copy.wait()

    send_idx_p = remote(couplings, idx_p, IDX_P, partner)
    send_idx_x = remote(couplings, idx_x, IDX_X, across)
    send_p0 = remote(slab0, win0.at[rows(PARTNER)], SLAB_P, partner)
    send_p1 = remote(slab1, win1.at[rows(PARTNER)], SLAB_P + 1, partner)
    send_a0 = remote(slab0, win0.at[rows(ACROSS)], SLAB_A, across)
    send_a1 = remote(slab1, win1.at[rows(ACROSS)], SLAB_A + 1, across)
    send_b0 = remote(slab0, win0.at[rows(ACROSS2)], SLAB_B, target2)
    send_b1 = remote(slab1, win1.at[rows(ACROSS2)], SLAB_B + 1, target2)
    send_f0 = remote(win0.at[rows(ACROSS)], win0.at[rows(FORWARDED)], SLAB_F, partner)
    send_f1 = remote(win1.at[rows(ACROSS)], win1.at[rows(FORWARDED)], SLAB_F + 1, partner)
    send_amp_p0 = remote(out_p0, amp_p0, AMP_P, partner)
    send_amp_p1 = remote(out_p1, amp_p1, AMP_P + 1, partner)
    send_amp_x0 = remote(out_x0, amp_x0, AMP_X, across)
    send_amp_x1 = remote(out_x1, amp_x1, AMP_X + 1, across)
    send_cur_p0 = remote(out_p0, cur_p0, CUR_P, partner)
    send_cur_p1 = remote(out_p1, cur_p1, CUR_P + 1, partner)
    send_cur_x0 = remote(out_x0, cur_x0, CUR_X, across)
    send_cur_x1a = remote(out_x1.at[:, pl.ds(0, CUT)], cur_x1a, CUR_X + 1, across)
    send_cur_x1b = remote(out_x1.at[:, pl.ds(CUT, nv - CUT)], cur_x1b, CUR_X_LAST, across)

    send_idx_x.start()
    send_idx_p.start()
    choose(sends_across, send_a0.start)
    choose(sends_two_across, send_b0.start)
    send_p0.start()
    send_p1.start()

    def tables(source, column, base):
        named = [source[column, p] - base for p in range(pairs)]
        present = []
        for q in range(pairs):
            hit = jnp.int32(0)
            for value in named:
                hit = jnp.maximum(hit, (value == q).astype(jnp.int32))
            present.append(hit)
        below = [jnp.int32(0)]
        for q in range(pairs - 1):
            below.append(below[-1] + present[q])
        return named, present, below

    for row, column, owner in ((0, column_p, partner), (1, column_x, across)):
        named, present, below = tables(couplings, column, owner * pairs)
        for p in range(pairs):
            value = jnp.int32(0)
            for q in range(pairs):
                value = value + jnp.where(named[p] == q, below[q], 0)
            slot[row, p] = jnp.minimum(value, picks - 1)

    send_idx_x.wait_recv()
    send_idx_p.wait_recv()
    for row, column, source in ((0, column_x, idx_p), (1, column_p, idx_x)):
        _, present, below = tables(source, column, me * pairs)
        for s in range(picks):
            value = jnp.int32(0)
            for q in range(pairs):
                chosen = jnp.logical_and(present[q] == 1, below[q] == s)
                value = value + jnp.where(chosen, q, 0)
            pick[row, s] = jnp.minimum(value, pairs - 1)

    def gather(row, dst, first):
        width = dst.shape[2]

        def step(s, carry):
            dst[s] = cur[pick[row, s], :, first : first + width]
            return carry

        lax.fori_loop(0, picks, step, 0)

    get_cur.wait()
    gather(1, out_x0, 0)
    gather(1, out_x1, CUT)
    send_amp_x0.start()
    send_amp_x1.start()
    choose(sends_across, send_a1.start)
    gather(0, out_p0, 0)
    gather(0, out_p1, CUT)
    send_amp_p0.start()
    send_amp_p1.start()

    def each_pair(step):
        def body(turn, carry):
            for p in range(PER_TURN):
                step(turn * PER_TURN + p)
            return carry

        lax.fori_loop(0, pairs // PER_TURN, body, 0)

    def third(p):
        return jnp.clip(couplings[2, p] - me * pairs, 0, pairs - 1)

    get_own.wait()

    def own_first(p):
        chosen = cur[third(p)]
        acc0[p] = transform(fock[2, p], inter_own[p], chosen, 0)

    each_pair(own_first)

    get_p.wait()
    send_amp_p0.wait_recv()
    send_amp_p1.wait_recv()

    def partner_first(p):
        q = slot[0, p]
        chosen = jnp.concatenate([amp_p0[q], amp_p1[q]], axis=1)
        acc0[p] += transform(fock[column_p, p], inter_p[p], chosen, 0)

    each_pair(partner_first)

    def second(p):
        offset = lax.div(pair_orbs[1, p], orbitals) - me
        parity = lax.rem(pair_orbs[1, p], orbitals)
        turned = offset * side
        place = jnp.where(turned >= 0, turned, 2 - turned)
        return jnp.clip(place * orbitals + parity, 0, win0.shape[0] - 1)

    def first_of(p):
        return jnp.clip(pair_orbs[0, p] - me * orbitals, 0, orbitals - 1)

    def forward0():
        send_a0.wait_recv()
        send_f0.start()

    choose(gets_across, forward0)
    get_left.wait()
    get_win0.wait()
    send_p0.wait_recv()
    choose(gets_across, send_b0.wait_recv, lambda: fill(slab0, win0, ACROSS, ACROSS2))
    choose(gets_forwarded, send_f0.wait_recv, lambda: fill(slab0, win0, FORWARDED))

    def integrals0(p):
        acc1[p, :, 0:CUT] = -slab_product(left[first_of(p)], win0[second(p)])

    each_pair(integrals0)

    get_x.wait()
    send_amp_x0.wait_recv()

    def across_first0(p):
        acc0[p] += transform(fock[column_x, p], inter_x[p], amp_x0[slot[1, p]], 0)

    each_pair(across_first0)

    send_amp_x1.wait_recv()
    choose(sends_two_across, send_b1.start)

    def across_first1(p):
        acc0[p] += transform(fock[column_x, p], inter_x[p], amp_x1[slot[1, p]], CUT)

    each_pair(across_first1)

    def denominator(p, first, width):
        row = virtual[pl.ds(p, 1), :]
        column = jnp.broadcast_to(row, (128, nv)).T
        if width > 128:
            column = jnp.concatenate([column] * (width // 128), axis=1)
        return column + row[:, first : first + width] - occupied[p]

    def update0(p):
        denom = denominator(p, 0, CUT)
        old = cur[p, :, 0:CUT]
        residual = denom * old - acc1[p, :, 0:CUT] - acc0[p, :, 0:CUT]
        cur[p, :, 0:CUT] = old - residual / denom

    each_pair(update0)

    send_amp_x0.wait_send()
    send_amp_x1.wait_send()
    send_amp_p0.wait_send()
    send_amp_p1.wait_send()
    gather(1, out_x0, 0)
    send_cur_x0.start()
    gather(0, out_p0, 0)
    send_cur_p0.start()

    def own_second0(p):
        chosen = cur[third(p), :, 0:CUT]
        whole = transform(fock[2, p], inter_own[p], chosen, 0)
        acc1[p, :, 0:CUT] += whole[:, 0:CUT]
        acc1[p, :, CUT:nv] = whole[:, CUT:nv]

    each_pair(own_second0)

    def forward1():
        send_a1.wait_recv()
        send_f1.start()

    choose(gets_across, forward1)
    send_cur_p0.wait_recv()

    def partner_second0(p):
        acc1[p] += transform(fock[column_p, p], inter_p[p], cur_p0[slot[0, p]], 0)

    each_pair(partner_second0)

    get_win1.wait()
    send_p1.wait_recv()
    choose(gets_across, send_b1.wait_recv, lambda: fill(slab1, win1, ACROSS, ACROSS2))
    choose(gets_forwarded, send_f1.wait_recv, lambda: fill(slab1, win1, FORWARDED))

    def update1(p):
        product = slab_product(left[first_of(p)], win1[second(p)])
        denom = denominator(p, CUT, nv - CUT)
        old = cur[p, :, CUT:nv]
        residual = product + denom * old - acc0[p, :, CUT:nv]
        cur[p, :, CUT:nv] = old - residual / denom
        acc1[p, :, CUT:nv] -= product

    each_pair(update1)

    gather(1, out_x1, CUT)
    send_cur_x1a.start()
    send_cur_x1b.start()
    gather(0, out_p1, CUT)
    send_cur_p1.start()

    def own_second1(p):
        chosen = cur[third(p), :, CUT:nv]
        acc1[p] += transform(fock[2, p], inter_own[p], chosen, CUT)

    each_pair(own_second1)

    send_cur_p1.wait_recv()

    def partner_second1(p):
        acc1[p] += transform(fock[column_p, p], inter_p[p], cur_p1[slot[0, p]], CUT)

    each_pair(partner_second1)

    send_cur_x0.wait_recv()

    def across_second0(p):
        acc1[p] += transform(fock[column_x, p], inter_x[p], cur_x0[slot[1, p]], 0)

    each_pair(across_second0)

    send_cur_x1a.wait_recv()

    def across_second1a(p):
        full_hi, full_lo = split(inter_x[p, :, 0:CUT])
        chunk_hi, chunk_lo = split(fock[column_x, p] * cur_x1a[slot[1, p]])
        halves[p] = narrow_half_upper(full_hi, full_lo, chunk_hi, chunk_lo)

    each_pair(across_second1a)

    send_cur_x1b.wait_recv()

    def across_second1b(p):
        full_hi, full_lo = split(inter_x[p, :, CUT:nv])
        chunk_hi, chunk_lo = split(fock[column_x, p] * cur_x1b[slot[1, p]])
        half = halves[p] + narrow_half_lower(full_hi, full_lo, chunk_hi, chunk_lo)
        whole = acc1[p] + second_product(half, full_hi, full_lo)
        denom = denominator(p, 0, nv)
        old = cur[p]
        cur[p] = old - (denom * old - whole) / denom

    each_pair(across_second1b)

    for copy in (
        send_idx_p,
        send_idx_x,
        send_p0,
        send_p1,
        send_cur_p0,
        send_cur_p1,
        send_cur_x0,
        send_cur_x1a,
        send_cur_x1b,
    ):
        copy.wait_send()

    def sent_across():
        send_a0.wait_send()
        send_a1.wait_send()

    def sent_two_across():
        send_b0.wait_send()
        send_b1.wait_send()

    def sent_forwarded():
        send_f0.wait_send()
        send_f1.wait_send()

    choose(sends_across, sent_across)
    choose(sends_two_across, sent_two_across)
    choose(gets_across, sent_forwarded)


def shards(
    slabs,
    amplitudes,
    intersections,
    fock_coupling,
    virt_energy,
    occ_pair_energy,
    pair_orbs,
    couplings,
):
    devices = lax.axis_size("orb")
    orbitals, nv, nq = slabs.shape
    pairs = amplitudes.shape[0]
    picks = pairs // 2
    smem = pl.BlockSpec(memory_space=pltpu.SMEM)
    vmem = pl.BlockSpec(memory_space=pltpu.VMEM)
    hbm = pl.BlockSpec(memory_space=pl.ANY)
    block = lambda count, width: pltpu.VMEM((count, nv, width), F32)
    pieces = [block(picks, CUT), block(picks, nv - CUT)]
    return pl.pallas_call(
        functools.partial(kernel, devices),
        out_shape=pltpu.VMEM(amplitudes.shape, F32),
        in_specs=[smem, smem, smem, smem, vmem, hbm, hbm, hbm],
        out_specs=vmem,
        scratch_shapes=[
            block(pairs, nv),
            block(pairs, nv),
            block(pairs, nv),
            block(pairs, nv),
            block(pairs, nv),
            block(orbitals, nq),
            pltpu.VMEM((5 * orbitals, CUT, nq), F32),
            pltpu.VMEM((5 * orbitals, nv - CUT, nq), F32),
            *(pieces * 3),
            pieces[0],
            pltpu.VMEM((picks, CUT, nv - CUT), F32),
            pltpu.VMEM((picks, nv - CUT, nv - CUT), F32),
            *(pieces * 2),
            pltpu.SMEM(couplings.shape[::-1], jnp.int32),
            pltpu.SMEM(couplings.shape[::-1], jnp.int32),
            pltpu.SMEM((2, picks), jnp.int32),
            pltpu.SMEM((2, pairs), jnp.int32),
            block(pairs, nv - CUT),
            pltpu.SemaphoreType.DMA((KINDS,)),
            pltpu.SemaphoreType.DMA((KINDS,)),
            pltpu.SemaphoreType.DMA((7,)),
            pltpu.SemaphoreType.DMA,
        ],
        compiler_params=pltpu.CompilerParams(
            collective_id=0, has_side_effects=True, vmem_limit_bytes=62000000
        ),
        name="amplitudes",
    )(
        couplings.T,
        pair_orbs.T,
        fock_coupling.T,
        occ_pair_energy,
        virt_energy,
        slabs,
        amplitudes,
        intersections,
    )


def solution(mesh):
    in_specs = (
        P("orb", None, None),
        P("orb", None, None),
        P("orb", None, None, None),
        P("orb", None),
        P("orb", None),
        P("orb"),
        P("orb", None),
        P("orb", None),
    )
    out_specs = P("orb", None, None)
    return jax.shard_map(shards, mesh=mesh, in_specs=in_specs, out_specs=out_specs, check_vma=False)
```

```python
import functools

import jax
import jax.numpy as jnp
from jax import lax
from jax.experimental import pallas as pl
from jax.experimental.pallas import tpu as pltpu
from jax.sharding import PartitionSpec as P

MESH = pl.DeviceIdType.MESH
F32 = jnp.float32
BF16 = jnp.bfloat16
NT = (((1,), (1,)), ((), ()))

CUT = 256

PER_TURN = 4

IDX_P, IDX_X = 0, 1
SLAB_P = 2
SLAB_A = 4
SLAB_B = 6
SLAB_F = 8
AMP_P = 10
AMP_X = 12
CUR_P = 14
CUR_X = 16
CUR_X_LAST = 18
KINDS = 19

OWN, PARTNER, FORWARDED, ACROSS, ACROSS2 = 0, 2, 4, 6, 8


def split(x):
    high = x.astype(BF16)
    return high, (x - high.astype(F32)).astype(BF16)


def dot_nn(a, b):
    return jnp.dot(a, b, preferred_element_type=F32)


def dot_nt(a, b):
    return lax.dot_general(a, b, NT, preferred_element_type=F32)


def by_halves(dot, a, b):
    middle = a.shape[0] // 2
    return jnp.concatenate([dot(a[:middle], b), dot(a[middle:], b)], axis=0)


def wide_half(full_hi, full_lo, chunk_hi, chunk_lo):
    return by_halves(
        dot_nn,
        jnp.concatenate([full_hi, full_hi, full_lo], axis=1),
        jnp.concatenate([chunk_hi, chunk_lo, chunk_hi], axis=0),
    )


def folded(product):
    width = product.shape[1] // 2
    return product[:, :width] + product[:, width:]


def narrow_half_upper(full_hi, full_lo, chunk_hi, chunk_lo):
    both = by_halves(dot_nn, full_hi, jnp.concatenate([chunk_hi, chunk_lo], axis=1))
    return folded(both) + by_halves(dot_nn, full_lo, chunk_hi)


def narrow_half_lower(full_hi, full_lo, chunk_hi, chunk_lo):
    upper = jnp.concatenate([chunk_hi, chunk_lo], axis=1)
    lower = jnp.concatenate([chunk_hi, jnp.zeros_like(chunk_lo)], axis=1)
    return folded(
        by_halves(
            dot_nn,
            jnp.concatenate([full_hi, full_lo], axis=1),
            jnp.concatenate([upper, lower], axis=0),
        )
    )


def second_product(half, part_hi, part_lo):
    half_hi, half_lo = split(half)
    return by_halves(
        dot_nt,
        jnp.concatenate([half_hi, half_hi, half_lo], axis=1),
        jnp.concatenate([part_hi, part_lo, part_hi], axis=1),
    )


def transform(gain, full, chunk, first):
    width = chunk.shape[1]
    full_hi, full_lo = split(full)
    chunk_hi, chunk_lo = split(gain * chunk)
    if width > 128:
        half = wide_half(full_hi, full_lo, chunk_hi, chunk_lo)
    else:
        half = narrow_half_upper(
            full_hi[:, :CUT], full_lo[:, :CUT], chunk_hi[:CUT], chunk_lo[:CUT]
        ) + narrow_half_lower(full_hi[:, CUT:], full_lo[:, CUT:], chunk_hi[CUT:], chunk_lo[CUT:])
    return second_product(
        half, full_hi[:, first : first + width], full_lo[:, first : first + width]
    )


def slab_product(left, right):
    left_hi, left_lo = split(left)
    right_hi, right_lo = split(right)
    return by_halves(
        dot_nt,
        jnp.concatenate([left_hi, left_hi, left_lo], axis=1),
        jnp.concatenate([right_hi, right_lo, right_hi], axis=1),
    )


def kernel(
    devices,
    couplings_hbm,
    pair_orbs_hbm,
    fock_hbm,
    occupied_hbm,
    virtual_hbm,
    slabs,
    amplitudes,
    intersections,
    acc1,
    inter_own,
    inter_x,
    halves,
    cur,
    couplings,
    pair_orbs,
    fock,
    occupied,
    virtual,
    acc0,
    inter_p,
    left,
    win0,
    win1,
    amp_p0,
    amp_p1,
    amp_x0,
    amp_x1,
    cur_p0,
    cur_p1,
    cur_x0,
    cur_x1a,
    cur_x1b,
    out_p0,
    out_p1,
    out_x0,
    out_x1,
    idx_p,
    idx_x,
    pick,
    slot,
    send_sem,
    recv_sem,
    local_sem,
    fill_sem,
):
    pairs, nv = cur.shape[0], cur.shape[1]
    picks = out_p0.shape[0]
    orbitals = left.shape[0]
    me = lax.axis_index("orb")
    side = 1 - 2 * lax.rem(me, 2)
    partner = me + side
    across = lax.rem(me - side + devices, devices)
    target2 = lax.rem(me + 2 * side + devices, devices)
    source2 = lax.rem(me - 2 * side + devices, devices)
    column_p = lax.rem(me + 1, 2)
    column_x = lax.rem(me, 2)

    sends_across = jnp.logical_and(me != devices - 1, me != 0)
    sends_two_across = jnp.logical_and(me != devices - 2, me != 1)
    gets_across = jnp.logical_and(me != 0, me != devices - 1)
    gets_forwarded = jnp.logical_and(me != 1, me != devices - 2)

    def choose(found, then, otherwise=None):
        pl.when(found)(then)
        if otherwise is not None:
            pl.when(jnp.logical_not(found))(otherwise)

    barrier = pltpu.get_barrier_semaphore()

    def greet(other):
        pl.semaphore_signal(barrier, inc=1, device_id=(other,), device_id_type=MESH)

    greet(partner)
    greet(across)
    choose(sends_two_across, lambda: greet(target2))
    choose(gets_across, lambda: greet(source2))
    local = []

    def fetch(src, dst):
        copy = pltpu.make_async_copy(src, dst, local_sem.at[len(local)])
        local.append(copy)
        copy.start()
        return copy

    get_couplings = fetch(couplings_hbm, couplings)
    get_cur = fetch(amplitudes, cur)

    greeted = 2 + sends_two_across.astype(jnp.int32) + gets_across.astype(jnp.int32)
    pl.semaphore_wait(barrier, greeted)

    def remote(src, dst, kind, device):
        return pltpu.make_async_remote_copy(
            src_ref=src,
            dst_ref=dst,
            send_sem=send_sem.at[kind],
            recv_sem=recv_sem.at[kind],
            device_id=(device,),
            device_id_type=MESH,
        )

    slab0 = slabs.at[:, pl.ds(0, CUT)]
    slab1 = slabs.at[:, pl.ds(CUT, nv - CUT)]
    rows = lambda first: pl.ds(first, orbitals)

    def fill(src, window, *places):
        for place in places:
            copy = pltpu.make_async_copy(src, window.at[rows(place)], fill_sem)
            copy.start()
            copy.wait()

    send_idx_p = remote(couplings_hbm, idx_p, IDX_P, partner)
    send_idx_x = remote(couplings_hbm, idx_x, IDX_X, across)
    send_p0 = remote(slab0, win0.at[rows(PARTNER)], SLAB_P, partner)
    send_p1 = remote(slab1, win1.at[rows(PARTNER)], SLAB_P + 1, partner)
    send_a0 = remote(slab0, win0.at[rows(ACROSS)], SLAB_A, across)
    send_a1 = remote(slab1, win1.at[rows(ACROSS)], SLAB_A + 1, across)
    send_b0 = remote(slab0, win0.at[rows(ACROSS2)], SLAB_B, target2)
    send_b1 = remote(slab1, win1.at[rows(ACROSS2)], SLAB_B + 1, target2)
    send_f0 = remote(win0.at[rows(ACROSS)], win0.at[rows(FORWARDED)], SLAB_F, partner)
    send_f1 = remote(win1.at[rows(ACROSS)], win1.at[rows(FORWARDED)], SLAB_F + 1, partner)
    send_amp_p0 = remote(out_p0, amp_p0, AMP_P, partner)
    send_amp_p1 = remote(out_p1, amp_p1, AMP_P + 1, partner)
    send_amp_x0 = remote(out_x0, amp_x0, AMP_X, across)
    send_amp_x1 = remote(out_x1, amp_x1, AMP_X + 1, across)
    send_cur_p0 = remote(out_p0, cur_p0, CUR_P, partner)
    send_cur_p1 = remote(out_p1, cur_p1, CUR_P + 1, partner)
    send_cur_x0 = remote(out_x0, cur_x0, CUR_X, across)
    send_cur_x1a = remote(out_x1.at[:, pl.ds(0, CUT)], cur_x1a, CUR_X + 1, across)
    send_cur_x1b = remote(out_x1.at[:, pl.ds(CUT, nv - CUT)], cur_x1b, CUR_X_LAST, across)

    send_idx_x.start()
    send_idx_p.start()
    choose(sends_across, send_a0.start)
    choose(sends_two_across, send_b0.start)
    send_p0.start()
    send_p1.start()

    get_own = fetch(intersections.at[:, 2], inter_own)
    get_p = fetch(intersections.at[:, column_p], inter_p)
    get_left = fetch(slabs, left)
    get_win0 = fetch(slabs.at[:, pl.ds(0, CUT)], win0.at[pl.ds(OWN, orbitals)])
    get_win1 = fetch(slabs.at[:, pl.ds(CUT, nv - CUT)], win1.at[pl.ds(OWN, orbitals)])
    get_x = fetch(intersections.at[:, column_x], inter_x)
    get_fock = fetch(fock_hbm, fock)
    get_pair_orbs = fetch(pair_orbs_hbm, pair_orbs)
    get_occupied = fetch(occupied_hbm, occupied)
    get_virtual = fetch(virtual_hbm, virtual)

    def tables(source, column, base):
        named = [source[column, p] - base for p in range(pairs)]
        present = []
        for q in range(pairs):
            hit = jnp.int32(0)
            for value in named:
                hit = jnp.maximum(hit, (value == q).astype(jnp.int32))
            present.append(hit)
        below = [jnp.int32(0)]
        for q in range(pairs - 1):
            below.append(below[-1] + present[q])
        return named, present, below

    get_couplings.wait()
    for row, column, owner in ((0, column_p, partner), (1, column_x, across)):
        named, present, below = tables(couplings, column, owner * pairs)
        for p in range(pairs):
            value = jnp.int32(0)
            for q in range(pairs):
                value = value + jnp.where(named[p] == q, below[q], 0)
            slot[row, p] = jnp.minimum(value, picks - 1)

    send_idx_x.wait_recv()
    send_idx_p.wait_recv()
    for row, column, source in ((0, column_x, idx_p), (1, column_p, idx_x)):
        _, present, below = tables(source, column, me * pairs)
        for s in range(picks):
            value = jnp.int32(0)
            for q in range(pairs):
                chosen = jnp.logical_and(present[q] == 1, below[q] == s)
                value = value + jnp.where(chosen, q, 0)
            pick[row, s] = jnp.minimum(value, pairs - 1)

    def gather(row, dst, first):
        width = dst.shape[2]

        def step(s, carry):
            dst[s] = cur[pick[row, s], :, first : first + width]
            return carry

        lax.fori_loop(0, picks, step, 0)

    get_cur.wait()
    gather(1, out_x0, 0)
    gather(1, out_x1, CUT)
    send_amp_x0.start()
    send_amp_x1.start()
    choose(sends_across, send_a1.start)
    gather(0, out_p0, 0)
    gather(0, out_p1, CUT)
    send_amp_p0.start()
    send_amp_p1.start()

    def each_pair(step):
        def body(turn, carry):
            for p in range(PER_TURN):
                step(turn * PER_TURN + p)
            return carry

        lax.fori_loop(0, pairs // PER_TURN, body, 0)

    def third(p):
        return jnp.clip(couplings[2, p] - me * pairs, 0, pairs - 1)

    get_own.wait()
    get_fock.wait()

    def own_first(p):
        chosen = cur[third(p)]
        acc0[p] = transform(fock[2, p], inter_own[p], chosen, 0)

    each_pair(own_first)

    get_p.wait()
    send_amp_p0.wait_recv()
    send_amp_p1.wait_recv()

    def partner_first(p):
        q = slot[0, p]
        chosen = jnp.concatenate([amp_p0[q], amp_p1[q]], axis=1)
        acc0[p] += transform(fock[column_p, p], inter_p[p], chosen, 0)

    each_pair(partner_first)

    def second(p):
        offset = lax.div(pair_orbs[1, p], orbitals) - me
        parity = lax.rem(pair_orbs[1, p], orbitals)
        turned = offset * side
        place = jnp.where(turned >= 0, turned, 2 - turned)
        return jnp.clip(place * orbitals + parity, 0, win0.shape[0] - 1)

    def first_of(p):
        return jnp.clip(pair_orbs[0, p] - me * orbitals, 0, orbitals - 1)

    def forward0():
        send_a0.wait_recv()
        send_f0.start()

    choose(gets_across, forward0)
    get_left.wait()
    get_pair_orbs.wait()
    get_win0.wait()
    send_p0.wait_recv()
    choose(gets_across, send_b0.wait_recv, lambda: fill(slab0, win0, ACROSS, ACROSS2))
    choose(gets_forwarded, send_f0.wait_recv, lambda: fill(slab0, win0, FORWARDED))

    def integrals0(p):
        acc1[p, :, 0:CUT] = -slab_product(left[first_of(p)], win0[second(p)])

    each_pair(integrals0)

    get_x.wait()
    send_amp_x0.wait_recv()

    def across_first0(p):
        acc0[p] += transform(fock[column_x, p], inter_x[p], amp_x0[slot[1, p]], 0)

    each_pair(across_first0)

    send_amp_x1.wait_recv()
    choose(sends_two_across, send_b1.start)

    def across_first1(p):
        acc0[p] += transform(fock[column_x, p], inter_x[p], amp_x1[slot[1, p]], CUT)

    each_pair(across_first1)

    def denominator(p, first, width):
        row = virtual[pl.ds(p, 1), :]
        column = jnp.broadcast_to(row, (128, nv)).T
        if width > 128:
            column = jnp.concatenate([column] * (width // 128), axis=1)
        return column + row[:, first : first + width] - occupied[p]

    def update0(p):
        denom = denominator(p, 0, CUT)
        old = cur[p, :, 0:CUT]
        residual = denom * old - acc1[p, :, 0:CUT] - acc0[p, :, 0:CUT]
        cur[p, :, 0:CUT] = old - residual / denom

    get_occupied.wait()
    get_virtual.wait()
    each_pair(update0)

    send_amp_x0.wait_send()
    send_amp_x1.wait_send()
    send_amp_p0.wait_send()
    send_amp_p1.wait_send()
    gather(1, out_x0, 0)
    send_cur_x0.start()
    gather(0, out_p0, 0)
    send_cur_p0.start()

    def own_second0(p):
        chosen = cur[third(p), :, 0:CUT]
        whole = transform(fock[2, p], inter_own[p], chosen, 0)
        acc1[p, :, 0:CUT] += whole[:, 0:CUT]
        acc1[p, :, CUT:nv] = whole[:, CUT:nv]

    each_pair(own_second0)

    def forward1():
        send_a1.wait_recv()
        send_f1.start()

    choose(gets_across, forward1)
    send_cur_p0.wait_recv()

    def partner_second0(p):
        acc1[p] += transform(fock[column_p, p], inter_p[p], cur_p0[slot[0, p]], 0)

    each_pair(partner_second0)

    get_win1.wait()
    send_p1.wait_recv()
    choose(gets_across, send_b1.wait_recv, lambda: fill(slab1, win1, ACROSS, ACROSS2))
    choose(gets_forwarded, send_f1.wait_recv, lambda: fill(slab1, win1, FORWARDED))

    def update1(p):
        product = slab_product(left[first_of(p)], win1[second(p)])
        denom = denominator(p, CUT, nv - CUT)
        old = cur[p, :, CUT:nv]
        residual = product + denom * old - acc0[p, :, CUT:nv]
        cur[p, :, CUT:nv] = old - residual / denom
        acc1[p, :, CUT:nv] -= product

    each_pair(update1)

    gather(1, out_x1, CUT)
    send_cur_x1a.start()
    send_cur_x1b.start()
    gather(0, out_p1, CUT)
    send_cur_p1.start()

    def own_second1(p):
        chosen = cur[third(p), :, CUT:nv]
        acc1[p] += transform(fock[2, p], inter_own[p], chosen, CUT)

    each_pair(own_second1)

    send_cur_p1.wait_recv()

    def partner_second1(p):
        acc1[p] += transform(fock[column_p, p], inter_p[p], cur_p1[slot[0, p]], CUT)

    each_pair(partner_second1)

    send_cur_x0.wait_recv()

    def across_second0(p):
        whole = acc1[p] + transform(fock[column_x, p], inter_x[p], cur_x0[slot[1, p]], 0)
        denom = denominator(p, 0, nv)
        inverse = 1.0 / denom
        old = cur[p]
        acc1[p] = old - (denom * old - whole) * inverse
        inter_own[p] = inverse

    each_pair(across_second0)

    send_cur_x1a.wait_recv()

    def across_second1a(p):
        full_hi, full_lo = split(inter_x[p, :, 0:CUT])
        chunk_hi, chunk_lo = split(fock[column_x, p] * cur_x1a[slot[1, p]])
        halves[p] = narrow_half_upper(full_hi, full_lo, chunk_hi, chunk_lo)

    each_pair(across_second1a)

    send_cur_x1b.wait_recv()

    def across_second1b(p):
        full_hi, full_lo = split(inter_x[p, :, CUT:nv])
        chunk_hi, chunk_lo = split(fock[column_x, p] * cur_x1b[slot[1, p]])
        halves[p] += narrow_half_lower(full_hi, full_lo, chunk_hi, chunk_lo)

    each_pair(across_second1b)

    for copy in (
        send_idx_p,
        send_idx_x,
        send_p0,
        send_p1,
        send_cur_p0,
        send_cur_p1,
        send_cur_x0,
        send_cur_x1a,
        send_cur_x1b,
    ):
        copy.wait_send()

    def sent_across():
        send_a0.wait_send()
        send_a1.wait_send()

    def sent_two_across():
        send_b0.wait_send()
        send_b1.wait_send()

    def sent_forwarded():
        send_f0.wait_send()
        send_f1.wait_send()

    choose(sends_across, sent_across)
    choose(sends_two_across, sent_two_across)
    choose(gets_across, sent_forwarded)


def finish(acc, inverse, inter, halves, out, held, sems):
    pairs = held.shape[0]

    def put(p):
        return pltpu.make_async_copy(held.at[p], out.at[p], sems.at[p])

    def body(turn, carry):
        for step in range(2):
            p = turn * 2 + step
            part_hi, part_lo = split(inter[p, :, CUT:])
            held[p] = acc[p] + second_product(halves[p], part_hi, part_lo) * inverse[p]
            put(p).start()
        return carry

    lax.fori_loop(0, pairs // 2, body, 0)
    for p in range(pairs):
        put(p).wait()


def shards(
    slabs,
    amplitudes,
    intersections,
    fock_coupling,
    virt_energy,
    occ_pair_energy,
    pair_orbs,
    couplings,
):
    devices = lax.axis_size("orb")
    orbitals, nv, nq = slabs.shape
    pairs = amplitudes.shape[0]
    picks = pairs // 2
    vmem = pl.BlockSpec(memory_space=pltpu.VMEM)
    hbm = pl.BlockSpec(memory_space=pl.ANY)
    block = lambda count, width: pltpu.VMEM((count, nv, width), F32)
    pieces = [block(picks, CUT), block(picks, nv - CUT)]
    kept = pl.pallas_call(
        functools.partial(kernel, devices),
        out_shape=[block(pairs, nv)] * 3 + [block(pairs, nv - CUT)],
        in_specs=[hbm] * 8,
        out_specs=[vmem] * 4,
        scratch_shapes=[
            block(pairs, nv),
            pltpu.SMEM(couplings.shape[::-1], jnp.int32),
            pltpu.SMEM(pair_orbs.shape[::-1], jnp.int32),
            pltpu.SMEM(fock_coupling.shape[::-1], F32),
            pltpu.SMEM(occ_pair_energy.shape, F32),
            pltpu.VMEM(virt_energy.shape, F32),
            block(pairs, nv),
            block(pairs, nv),
            block(orbitals, nq),
            pltpu.VMEM((5 * orbitals, CUT, nq), F32),
            pltpu.VMEM((5 * orbitals, nv - CUT, nq), F32),
            *(pieces * 3),
            pieces[0],
            pltpu.VMEM((picks, CUT, nv - CUT), F32),
            pltpu.VMEM((picks, nv - CUT, nv - CUT), F32),
            *(pieces * 2),
            pltpu.SMEM(couplings.shape[::-1], jnp.int32),
            pltpu.SMEM(couplings.shape[::-1], jnp.int32),
            pltpu.SMEM((2, picks), jnp.int32),
            pltpu.SMEM((2, pairs), jnp.int32),
            pltpu.SemaphoreType.DMA((KINDS,)),
            pltpu.SemaphoreType.DMA((KINDS,)),
            pltpu.SemaphoreType.DMA((12,)),
            pltpu.SemaphoreType.DMA,
        ],
        compiler_params=pltpu.CompilerParams(
            collective_id=0, has_side_effects=True, vmem_limit_bytes=51300000
        ),
        name="amplitudes",
    )(
        couplings.T,
        pair_orbs.T,
        fock_coupling.T,
        occ_pair_energy,
        virt_energy,
        slabs,
        amplitudes,
        intersections,
    )
    return pl.pallas_call(
        finish,
        out_shape=jax.ShapeDtypeStruct(amplitudes.shape, F32),
        in_specs=[vmem] * 4,
        out_specs=hbm,
        scratch_shapes=[block(pairs, nv), pltpu.SemaphoreType.DMA((pairs,))],
        compiler_params=pltpu.CompilerParams(vmem_limit_bytes=32 << 20),
        name="finish",
    )(*kept)


def solution(mesh):
    in_specs = (
        P("orb", None, None),
        P("orb", None, None),
        P("orb", None, None, None),
        P("orb", None),
        P("orb", None),
        P("orb"),
        P("orb", None),
        P("orb", None),
    )
    out_specs = P("orb", None, None)
    return jax.shard_map(shards, mesh=mesh, in_specs=in_specs, out_specs=out_specs, check_vma=False)
```
